512 devices in a mesh: grp: 16 (over z, core), blk: 32 (over y, x).
Axes of the slice: x: 4, y: 8, z: 8, core: 2. Of those that a mesh axis runs over, the one named last changes fastest.
Arguments:
- integrals: bfloat16 [32, 2048, 2048], P('blk', None, 'grp'), as said below
- tile_mask: int32 [16, 16], replicated, may hold values from 0 to 1, as said below
- tile_owner: int32 [16], replicated, may hold values from 0 to 15, as said below
- occupied_tiles: bfloat16 [16384, 128], P(('grp', 'blk')), may hold values from -0.1875 to 0.1875
- occupied_offsets: int32 [8], replicated, may hold values from 0 to 15, as said below
- virtual_tiles: bfloat16 [16384, 128], P(('grp', 'blk')), may hold values from -0.1875 to 0.1875
- virtual_offsets: int32 [8], replicated, may hold values from 0 to 15, as said below
Outputs:
- polarizability: float32 [32, 32], P('blk')
The draws below stay inside these ranges and needn't reach their ends.
Inputs may be any that keep to these rules, and one draw needn't show every extreme that they name: `integrals`: after column slot s is placed at basis tile tile_owner[s], the tensor is symmetric in its two basis indices. `tile_mask`: symmetric, with ones on the diagonal. `tile_owner`: each tile exactly once. `occupied_offsets`: 8 different tile offsets, among them 0 and 15. `virtual_offsets`: 8 different tile offsets, among them 0 and 15.
All inputs are finite; a program needn't handle non-finite values.
Results may differ from the reference program's by a relative error of at most 0.004.
Values may be sent and summed in bfloat16 or wider, within the bound.
A program may use at most 64 MiB of HBM per device.

```python
import jax
import jax.numpy as jnp
from jax import lax

TW = 128
NT = 16
K = 8
NAUX = 32
NAO = 2048


def owner_order(key):
    return jax.random.permutation(jax.random.fold_in(key, 11), NT).astype(jnp.int32)


def mask_table(key):
    coins = jax.random.randint(jax.random.fold_in(key, 12), (NT, NT), 0, 5)
    upper = jnp.triu((coins < 3).astype(jnp.int32), 1)
    return upper + upper.T + jnp.eye(NT, dtype=jnp.int32)


def offset_set(key):
    middle = 1 + jax.random.permutation(jax.random.fold_in(key, 1), NT - 2)[:K - 2].astype(jnp.int32)
    ends = jnp.array([0, NT - 1], dtype=jnp.int32)
    values = jnp.concatenate([ends, middle]).astype(jnp.int32)
    order = jax.random.permutation(jax.random.fold_in(key, 2), K).astype(jnp.int32)
    return values[order].astype(jnp.int32)


def draw_tile_owner(key, part):
    return owner_order(key)


def draw_tile_mask(key, part):
    return mask_table(key)


def draw_integrals(key, part):
    order = owner_order(key)
    base_key = jax.random.fold_in(key, 13)

    def one_row(index):
        row_key = jax.random.fold_in(base_key, index)
        raw_values = jax.random.normal(row_key, (NAO, NAO), jnp.float32)
        factor = jnp.float32(1.0)
        symmetric = (raw_values + raw_values.T) * (0.7071 * factor)
        placed = symmetric.reshape(NAO, NT, TW)[:, order, :]
        return placed.reshape(NAO, NAO)
    return lax.map(one_row, jnp.arange(NAUX)).astype(jnp.bfloat16)


def draw_occupied_offsets(key, part):
    return offset_set(jax.random.fold_in(key, 21))


def draw_virtual_offsets(key, part):
    return offset_set(jax.random.fold_in(key, 22))


def levels(stream_key, extent, pieces, smallest, largest):
    level = 1.0
    for axis_at, parts in pieces:
        steps = jax.random.uniform(jax.random.fold_in(jax.random.fold_in(stream_key, 6), axis_at), (parts,), jnp.float32, smallest / len(pieces), largest / len(pieces))
        level = level * jnp.repeat(jnp.exp(steps), extent[axis_at] // parts).reshape((-1,) + (1,) * (len(extent) - 1 - axis_at))
    return level


def bell_draw(rng, shape, width, reach, shards=(), kind=jnp.bfloat16):
    gain = levels(rng, shape, shards, -0.22, 0.18) if shards else 1.0
    values = jax.random.normal(rng, shape, jnp.float32) * width * gain
    return jnp.minimum(jnp.maximum(values, -reach), reach).astype(kind)


def setup_inputs(seed: int = 0) -> dict:
    keys = jax.random.split(jax.random.key(seed), 8)
    return {
        "integrals": draw_integrals(jax.random.fold_in(keys[7], 71), 0),
        "tile_mask": draw_tile_mask(jax.random.fold_in(keys[7], 71), 0),
        "tile_owner": draw_tile_owner(jax.random.fold_in(keys[7], 71), 0),
        "occupied_tiles": bell_draw(keys[3], (NT * K * TW, TW), (K * TW) ** -0.5, 0.1875, ((0, 512),)),
        "occupied_offsets": draw_occupied_offsets(jax.random.fold_in(keys[7], 71), 0),
        "virtual_tiles": bell_draw(keys[5], (NT * K * TW, TW), (K * TW) ** -0.5, 0.1875, ((0, 512),)),
        "virtual_offsets": draw_virtual_offsets(jax.random.fold_in(keys[7], 71), 0),
    }


def column_block(integrals, tile_mask, slot_of, tile_index):
    slot = slot_of[tile_index].astype(jnp.int32)
    block = lax.dynamic_slice_in_dim(integrals, (slot * TW).astype(jnp.int32), TW, 2)
    weights = jnp.repeat(tile_mask[:, tile_index], TW).astype(jnp.float32)
    return block.astype(jnp.float32) * weights[None, :, None]


def rounded(values):
    return lax.optimization_barrier(values.astype(jnp.bfloat16)).astype(jnp.float32)


def reference(integrals, tile_mask, tile_owner, occupied_tiles, occupied_offsets, virtual_tiles, virtual_offsets):
    slot_of = jnp.zeros((NT,), jnp.int32).at[tile_owner].set(jnp.arange(NT, dtype=jnp.int32))
    occupied = occupied_tiles.astype(jnp.float32).reshape(NT, K, TW, TW)
    virtual = virtual_tiles.astype(jnp.float32).reshape(NT, K, TW, TW)
    targets = jnp.arange(NT, dtype=jnp.int32)
    sources = ((targets[:, None] - occupied_offsets[None, :]) % NT).astype(jnp.int32)
    picked = occupied[sources, jnp.arange(K, dtype=jnp.int32)[None, :]]

    def one_tile(tile_index, total):
        block = column_block(integrals, tile_mask, slot_of, tile_index)
        tiled = block.reshape(NAUX, NT, TW, TW)
        occupied_half = jnp.zeros((NAUX, NT, TW, TW), jnp.float32)
        virtual_half = jnp.zeros((NAUX, NAO, TW), jnp.float32)
        virtual_rows = lax.dynamic_index_in_dim(virtual, tile_index, 0, keepdims=False)
        for slot in range(K):
            inputs = jnp.take(tiled, sources[:, slot], axis=1)
            occupied_half = occupied_half + jnp.einsum("kmn,pkml->pknl", picked[:, slot], inputs, precision=lax.Precision.HIGHEST)
            partner = ((tile_index + virtual_offsets[slot]) % NT).astype(jnp.int32)
            other = column_block(integrals, tile_mask, slot_of, partner)
            virtual_half = virtual_half + jnp.einsum("pvm,nm->pvn", other, virtual_rows[slot], precision=lax.Precision.HIGHEST)
        left_side = rounded(occupied_half).reshape(NAUX, NAO * TW)
        right_side = rounded(virtual_half).reshape(NAUX, NAO * TW)
        return total + jnp.dot(left_side, right_side.T, precision=lax.Precision.HIGHEST, preferred_element_type=jnp.float32)

    total = lax.fori_loop(0, NT, one_tile, jnp.zeros((NAUX, NAUX), jnp.float32))
    return total / NAO
```

```python
import functools

import jax
import jax.numpy as jnp
from jax import lax
from jax.experimental import pallas as pl
from jax.experimental.pallas import tpu as pltpu
from jax.sharding import PartitionSpec as P

MESH = pl.DeviceIdType.MESH
TW = 128
F32 = jnp.float32
BF16 = jnp.bfloat16


class Dims:
    def __init__(self, ng, nb, x, kcount):
        self.C = 2
        self.NG, self.NB = ng, nb
        self.Z, self.X, self.Y = ng // 2, x, nb // x
        self.NT, self.K = ng, kcount
        self.RPD = kcount * TW // nb
        self.CH = ng * TW // nb
        self.HP = TW // self.CH


def ring_plan(n, nsub):
    plan = []
    for k in range(1, n // 2 + 1):
        for sub in range(nsub):
            last = 2 * k == n
            if not last:
                plan += [(1, k, sub), (-1, k, sub)]
            else:
                plan.append((1 if sub < (nsub + 1) // 2 else -1, k, sub))
    return plan


class Sems:
    def __init__(self):
        self.count = 0

    def take(self, n=1):
        base = self.count
        self.count += n
        return base


def layout(d, nsub):
    s = Sems()
    t = {}
    for name in ("o", "v"):
        t["x" + name] = s.take(d.X)
    mid = {"o": d.Y, "v": d.Z}
    last = {"o": d.Z, "v": d.Y}
    for name in ("o", "v"):
        t["mid" + name] = {e: s.take() for e in ring_plan(mid[name], 1)}
        t["last" + name] = {e: s.take() for e in ring_plan(last[name], nsub)}
        t["sib" + name] = {e: s.take() for e in ring_plan(last[name], nsub)}
        t["own" + name] = s.take()
    t["R"] = s.take(d.NB)
    t["Lg"] = s.take(d.NG)
    t["Lb"] = s.take(d.NB)
    t["S1"] = s.take(d.NB)
    t["S2"] = s.take(d.NG)
    return t, s.count


def kernel(
    d,
    nsub,
    t,
    mask_ref,
    owner_ref,
    ooff_ref,
    voff_ref,
    b_ref,
    ot_ref,
    vt_ref,
    out_ref,
    go,
    gv,
    bm,
    bt,
    rbuf,
    rb,
    lbuf,
    lg,
    lb,
    s1,
    s1r,
    s2,
    ssem,
    rsem,
):
    g = lax.axis_index("grp")
    b = lax.axis_index("blk")
    z, c = g // 2, lax.rem(g, 2)
    y, x = b // d.X, lax.rem(b, d.X)
    sib = z * 2 + (1 - c)

    def rcopy(src, dst, i, j, gg, bb):
        return pltpu.make_async_remote_copy(
            src_ref=src,
            dst_ref=dst,
            send_sem=ssem.at[i],
            recv_sem=rsem.at[j],
            device_id=(gg, bb),
            device_id_type=MESH,
        )

    barrier = pltpu.get_barrier_semaphore()

    @pl.loop(1, d.NG)
    def _(k):
        pl.semaphore_signal(
            barrier, inc=1, device_id=(lax.rem(g + k, d.NG), b), device_id_type=MESH
        )

    @pl.loop(1, d.NB)
    def _(k):
        pl.semaphore_signal(
            barrier, inc=1, device_id=(g, lax.rem(b + k, d.NB)), device_id_type=MESH
        )

    go[z, c, y, x] = ot_ref[...]
    gv[z, c, y, x] = vt_ref[...]
    pl.semaphore_wait(barrier, d.NG + d.NB - 2)

    bufs = {"o": go, "v": gv}
    sends = []

    for k in range(1, d.X):
        for name in ("o", "v"):
            ref = bufs[name].at[z, c, y, x]
            i = t["x" + name] + k
            cp = rcopy(ref, ref, i, i, g, y * d.X + lax.rem(x + k, d.X))
            cp.start()
            sends.append(cp)

    own = owner_ref[g]

    @pl.loop(0, d.NT)
    def _(i):
        m = mask_ref[i, own].astype(F32)
        tile = (b_ref[0, pl.ds(pl.multiple_of(i * TW, TW), TW), :].astype(F32) * m).astype(BF16)
        bm[i] = tile
        bt[i] = tile.T

    for k in range(1, d.X):
        for name in ("o", "v"):
            ref = bufs[name].at[z, c, y, lax.rem(x - k + d.X, d.X)]
            i = t["x" + name] + k
            rcopy(ref, ref, i, i, g, b).wait_recv()

    def along_z(k):
        return lax.rem(z + k + d.Z, d.Z) * 2 + c, b

    def along_y(k):
        return g, lax.rem(y + k + d.Y, d.Y) * d.X + x

    def pos_z(k):
        return lax.rem(z + k + d.Z, d.Z)

    def pos_y(k):
        return lax.rem(y + k + d.Y, d.Y)

    def mid_block(name, off):
        if name == "o":
            return go.at[z, c, pos_y(off)]
        return gv.at[pos_z(off), c, y]

    def last_block(name, off, sub, core):
        if name == "o":
            h = d.Y // nsub
            return go.at[pos_z(off), core, pl.ds(sub * h, h)]
        h = d.Z // nsub
        return gv.at[pl.ds(sub * h, h), core, pos_y(off)]

    mid_axis = {"o": along_y, "v": along_z}
    last_axis = {"o": along_z, "v": along_y}

    def run(stage, sizes, axis, block, nsubs, forward):
        plans = {name: ring_plan(sizes[name], nsubs) for name in ("o", "v")}

        def send(name, e):
            dirn, k, sub = e
            ref = block(name, -dirn * (k - 1), sub)
            i = t[stage + name][e]
            cp = rcopy(ref, ref, i, i, *axis[name](dirn))
            cp.start()
            sends.append(cp)

        for name in ("o", "v"):
            for e in plans[name]:
                if e[1] == 1:
                    send(name, e)
        if forward:
            for name in ("o", "v"):
                forward(name, None)
        order = []
        for n in range(max(len(plans["o"]), len(plans["v"]))):
            for name in ("v", "o"):
                if n < len(plans[name]):
                    order.append((name, plans[name][n]))
        for name, e in order:
            dirn, k, sub = e
            ref = block(name, -dirn * k, sub)
            i = t[stage + name][e]
            rcopy(ref, ref, i, i, g, b).wait_recv()
            nxt = (dirn, k + 1, sub)
            if nxt in plans[name]:
                send(name, nxt)
            if forward:
                forward(name, e)

    def sibling(name, e):
        if e is None:
            ref = go.at[z, c] if name == "o" else gv.at[:, c, y]
            i = t["own" + name]
        else:
            dirn, k, sub = e
            ref = last_block(name, -dirn * k, sub, c)
            i = t["sib" + name][e]
        cp = rcopy(ref, ref, i, i, sib, b)
        cp.start()
        sends.append(cp)

    def from_sibling(name):
        ref = go.at[z, 1 - c] if name == "o" else gv.at[:, 1 - c, y]
        i = t["own" + name]
        rcopy(ref, ref, i, i, g, b).wait_recv()
        n = d.Z if name == "o" else d.Y
        for e in ring_plan(n, nsub):
            dirn, k, sub = e
            ref = last_block(name, -dirn * k, sub, 1 - c)
            i = t["sib" + name][e]
            rcopy(ref, ref, i, i, g, b).wait_recv()

    run(
        "mid",
        {"o": d.Y, "v": d.Z},
        mid_axis,
        lambda name, off, sub: mid_block(name, off),
        1,
        None,
    )
    run(
        "last",
        {"o": d.Z, "v": d.Y},
        last_axis,
        lambda name, off, sub: last_block(name, off, sub, c),
        nsub,
        sibling,
    )
    from_sibling("v")

    def tiles_of(ref, i):
        return ref[i // 2, lax.rem(i, 2)].reshape(d.K, TW, TW)

    @pl.loop(0, d.NT)
    def _(kk):
        j = lax.rem(b // d.HP + kk, d.NT)
        row = owner_ref[j]
        tiles = tiles_of(gv, row)
        left = jnp.concatenate([tiles[s] for s in range(d.K)], axis=1)
        right = jnp.concatenate(
            [bm[lax.rem(row + voff_ref[s], d.NT)] for s in range(d.K)], axis=0
        )
        value = jnp.dot(left, right, preferred_element_type=F32).astype(BF16)
        for h in range(d.HP):
            to = j * d.HP + h
            rbuf[to] = value[h * d.CH : (h + 1) * d.CH]

            @pl.when(to != b)
            def _():
                rcopy(rbuf.at[to], rb.at[b], t["R"] + to, t["R"] + b, g, to).start()

            @pl.when(to == b)
            def _():
                rb[b] = value[h * d.CH : (h + 1) * d.CH]

    from_sibling("o")

    @pl.loop(0, d.NT)
    def _(kk):
        j = lax.rem(g + kk, d.NT)
        col = owner_ref[j]
        lefts, rights = [], []
        for s in range(d.K):
            i = lax.rem(col - ooff_ref[s] + d.NT, d.NT)
            lefts.append(bt[i])
            per = d.NB // d.K
            rows = go[i // 2, lax.rem(i, 2)].reshape(d.K, TW, TW)[s]
            rights.append(rows)
        value = jnp.dot(
            jnp.concatenate(lefts, axis=1),
            jnp.concatenate(rights, axis=0),
            preferred_element_type=F32,
        ).astype(BF16)
        lbuf[j] = value

        @pl.when(j != g)
        def _():
            rcopy(lbuf.at[j], lg.at[g], t["Lg"] + j, t["Lg"] + g, j, b).start()

        @pl.when(j == g)
        def _():
            lg[g] = value

    @pl.loop(0, d.NT)
    def _(kk):
        j = lax.rem(g - kk + d.NT, d.NT)

        @pl.when(j != g)
        def _():
            rcopy(lg.at[j], lg.at[j], t["Lg"] + j, t["Lg"] + j, j, b).wait_recv()

        for h in range(d.HP):
            to = j * d.HP + h
            src = lg.at[j, pl.ds(h * d.CH, d.CH)]

            @pl.when(to != b)
            def _():
                rcopy(src, lb.at[b], t["Lb"] + to, t["Lb"] + b, g, to).start()

            @pl.when(to == b)
            def _():
                lb[b] = src[...]

    @pl.loop(1, d.NB)
    def _(k):
        q = lax.rem(b + k, d.NB)
        rcopy(rb.at[q], rb.at[q], t["R"] + q, t["R"] + q, g, q).wait_recv()

    @pl.loop(1, d.NB)
    def _(k):
        q = lax.rem(b + k, d.NB)
        rcopy(lb.at[q], lb.at[q], t["Lb"] + q, t["Lb"] + q, g, q).wait_recv()

    n16 = d.NB * 16
    prod = jnp.zeros((n16, n16), F32)
    for r in range(d.CH // 16):
        left = lb[:, 16 * r : 16 * r + 16, :].reshape(n16, TW)
        right = rb[:, 16 * r : 16 * r + 16, :].reshape(n16, TW)
        prod = prod + lax.dot_general(
            left, right, (((1,), (1,)), ((), ())), preferred_element_type=F32
        )
    ii = lax.broadcasted_iota(jnp.int32, (n16, n16), 0)
    jj = lax.broadcasted_iota(jnp.int32, (n16, n16), 1)
    prod = jnp.where((ii & 15) == (jj & 15), prod, 0.0)
    folded = jnp.sum(prod.reshape(d.NB, 16, n16), axis=1)
    pick = (
        lax.broadcasted_iota(jnp.int32, (n16, TW), 0) // 16
        == lax.broadcasted_iota(jnp.int32, (n16, TW), 1)
    ).astype(F32)
    part = jnp.dot(
        folded, pick, precision=lax.Precision.HIGHEST, preferred_element_type=F32
    )
    s1[...] = jnp.broadcast_to(part[:, None, :], (d.NB, 8, TW))
    s1r[b] = s1[b]

    @pl.loop(1, d.NB)
    def _(k):
        q = lax.rem(b + k, d.NB)
        rcopy(s1.at[q], s1r.at[b], t["S1"] + q, t["S1"] + b, g, q).start()

    @pl.loop(1, d.NB)
    def _(k):
        q = lax.rem(b + k, d.NB)
        rcopy(s1r.at[q], s1r.at[q], t["S1"] + q, t["S1"] + q, g, q).wait_recv()

    s2[g] = jnp.sum(s1r[...], axis=0)

    @pl.loop(1, d.NG)
    def _(k):
        q = lax.rem(g + k, d.NG)
        rcopy(s2.at[g], s2.at[g], t["S2"] + q, t["S2"] + g, q, b).start()

    @pl.loop(1, d.NG)
    def _(k):
        q = lax.rem(g + k, d.NG)
        rcopy(s2.at[q], s2.at[q], t["S2"] + q, t["S2"] + q, q, b).wait_recv()

    total = jnp.sum(s2[...], axis=0)
    out_ref[...] = total[0:1, : d.NB] * (1.0 / (d.NT * TW))

    for cp in sends:
        cp.wait_send()

    @pl.loop(1, d.NB)
    def _(k):
        q = lax.rem(b + k, d.NB)
        rcopy(rbuf.at[q], rbuf.at[q], t["R"] + q, t["R"] + q, g, q).wait_send()
        rcopy(rbuf.at[q], rbuf.at[q], t["Lb"] + q, t["Lb"] + q, g, q).wait_send()
        rcopy(s1.at[q], s1.at[q], t["S1"] + q, t["S1"] + q, g, q).wait_send()

    @pl.loop(1, d.NG)
    def _(k):
        q = lax.rem(g + k, d.NG)
        rcopy(lbuf.at[q], lbuf.at[q], t["Lg"] + q, t["Lg"] + q, q, b).wait_send()
        rcopy(s2.at[q], s2.at[q], t["S2"] + q, t["S2"] + q, q, b).wait_send()


def make(d, nsub):
    t, nsem = layout(d, nsub)

    def body(integrals, mask, owner, otiles, ooff, vtiles, voff):
        vmem = pl.BlockSpec(memory_space=pltpu.VMEM)
        smem = pl.BlockSpec(memory_space=pltpu.SMEM)
        gshape = (d.Z, 2, d.Y, d.X, d.RPD, TW)
        return pl.pallas_call(
            functools.partial(kernel, d, nsub, t),
            out_shape=jax.ShapeDtypeStruct((1, d.NB), F32),
            in_specs=[smem] * 4 + [vmem] * 3,
            out_specs=vmem,
            scratch_shapes=[
                pltpu.VMEM(gshape, BF16),
                pltpu.VMEM(gshape, BF16),
                pltpu.VMEM((d.NT, TW, TW), BF16),
                pltpu.VMEM((d.NT, TW, TW), BF16),
                pltpu.VMEM((d.NB, d.CH, TW), BF16),
                pltpu.VMEM((d.NB, d.CH, TW), BF16),
                pltpu.VMEM((d.NT, TW, TW), BF16),
                pltpu.VMEM((d.NT, TW, TW), BF16),
                pltpu.VMEM((d.NB, d.CH, TW), BF16),
                pltpu.VMEM((d.NB, 8, TW), F32),
                pltpu.VMEM((d.NB, 8, TW), F32),
                pltpu.VMEM((d.NG, 8, TW), F32),
                pltpu.SemaphoreType.DMA((nsem,)),
                pltpu.SemaphoreType.DMA((nsem,)),
            ],
            compiler_params=pltpu.CompilerParams(
                collective_id=0, has_side_effects=True, vmem_limit_bytes=40 << 20
            ),
        )(mask, owner, ooff, voff, integrals, otiles, vtiles)

    return body


def solution(mesh, x=4, kcount=8, nsub=2):
    d = Dims(mesh.shape["grp"], mesh.shape["blk"], x, kcount)
    in_specs = (
        P("blk", None, "grp"),
        P(),
        P(),
        P(("grp", "blk"), None),
        P(),
        P(("grp", "blk"), None),
        P(),
    )
    return jax.shard_map(
        make(d, nsub), mesh=mesh, in_specs=in_specs, out_specs=P("blk", None), check_vma=False
    )
```

```python
import functools

import jax
import jax.numpy as jnp
from jax import lax
from jax.experimental import pallas as pl
from jax.experimental.pallas import tpu as pltpu
from jax.sharding import PartitionSpec as P

MESH = pl.DeviceIdType.MESH
TW = 128
F32 = jnp.float32
BF16 = jnp.bfloat16


class Dims:
    def __init__(self, ng, nb, x, kcount):
        self.C = 2
        self.NG, self.NB = ng, nb
        self.Z, self.X, self.Y = ng // 2, x, nb // x
        self.NT, self.K = ng, kcount
        self.RPD = kcount * TW // nb
        self.CH = ng * TW // nb
        self.HP = TW // self.CH


def ring_plan(n, nsub):
    plan = []
    for k in range(1, n // 2 + 1):
        for sub in range(nsub):
            last = 2 * k == n
            if not last:
                plan += [(1, k, sub), (-1, k, sub)]
            else:
                plan.append((1 if sub < (nsub + 1) // 2 else -1, k, sub))
    return plan


class Sems:
    def __init__(self):
        self.count = 0

    def take(self, n=1):
        base = self.count
        self.count += n
        return base


def layout(d, nsub):
    s = Sems()
    t = {}
    last = {"o": d.Z, "v": d.Y}
    for name in ("o", "v"):
        t["last" + name] = {e: s.take() for e in ring_plan(last[name], nsub)}
        t["sib" + name] = {e: s.take() for e in ring_plan(last[name], nsub)}
        t["own" + name] = s.take()
    t["R"] = s.take(d.NB)
    t["Lg"] = s.take(d.NG)
    t["Lb"] = s.take(d.NB)
    t["S1"] = s.take(d.NB)
    t["S2"] = s.take(d.NG)
    t["Po"] = s.take(d.Y * d.X)
    t["Pv"] = s.take(d.Z * d.X)
    t["in"] = s.take(7)
    return t, s.count


def kernel(
    d,
    nsub,
    t,
    mask_hbm,
    owner_hbm,
    ooff_hbm,
    voff_hbm,
    b_hbm,
    ot_ref,
    vt_ref,
    out_ref,
    mask_ref,
    owner_ref,
    ooff_ref,
    voff_ref,
    b_ref,
    go,
    gv,
    bm,
    bt,
    rbuf,
    rb,
    lbuf,
    lg,
    lb,
    s1,
    s1r,
    s2,
    ssem,
    rsem,
):
    g = lax.axis_index("grp")
    b = lax.axis_index("blk")
    z, c = g // 2, lax.rem(g, 2)
    y, x = b // d.X, lax.rem(b, d.X)
    sib = z * 2 + (1 - c)

    def rcopy(src, dst, i, j, gg, bb):
        return pltpu.make_async_remote_copy(
            src_ref=src,
            dst_ref=dst,
            send_sem=ssem.at[i],
            recv_sem=rsem.at[j],
            device_id=(gg, bb),
            device_id_type=MESH,
        )

    barrier = pltpu.get_barrier_semaphore()

    def signal(gg, bb):
        pl.semaphore_signal(barrier, inc=1, device_id=(gg, bb), device_id_type=MESH)

    @pl.loop(1, d.NG)
    def _(k):
        signal(lax.rem(g + k, d.NG), b)

    @pl.loop(1, d.NB)
    def _(k):
        signal(g, lax.rem(b + k, d.NB))

    for dx in range(1, d.X):

        @pl.loop(1, d.Z)
        def _(k):
            signal(lax.rem(z + k, d.Z) * 2 + c, y * d.X + lax.rem(x + dx, d.X))

    loads = [
        pltpu.make_async_copy(src, dst, ssem.at[t["in"] + i])
        for i, (src, dst) in enumerate(
            [
                (ot_ref, go.at[z, c, y, x]),
                (vt_ref, gv.at[z, c, y, x]),
                (mask_hbm, mask_ref),
                (owner_hbm, owner_ref),
                (ooff_hbm, ooff_ref),
                (voff_hbm, voff_ref),
                (b_hbm, b_ref),
            ]
        )
    ]
    for cp in loads:
        cp.start()
    pl.semaphore_wait(barrier, d.NG + d.NB - 2 + (d.X - 1) * (d.Z - 1))

    sends = []

    def plane_copy(name, k, incoming):
        sign = -1 if incoming else 1
        dx = lax.rem(k, d.X)
        xx = lax.rem(x + sign * dx + d.X, d.X)
        if name == "o":
            yy = lax.rem(y + sign * (k // d.X) + d.Y, d.Y)
            dst = go.at[z, c, yy, xx] if incoming else go.at[z, c, y, x]
            src, to = ot_ref, (g, yy * d.X + xx)
        else:
            zz = lax.rem(z + sign * (k // d.X) + d.Z, d.Z)
            dst = gv.at[zz, c, y, xx] if incoming else gv.at[z, c, y, x]
            src, to = vt_ref, (zz * 2 + c, y * d.X + xx)
        i = t["P" + name] + k
        return rcopy(dst if incoming else src, dst, i, i, *to)

    plane = {"o": d.Y * d.X, "v": d.Z * d.X}
    for name in ("o", "v"):

        @pl.loop(1, plane[name])
        def _(k):
            plane_copy(name, k, False).start()

    for cp in loads:
        cp.wait()

    own = owner_ref[g]

    @pl.loop(0, d.NT)
    def _(i):
        m = mask_ref[i, own].astype(F32)
        tile = (b_ref[0, pl.ds(pl.multiple_of(i * TW, TW), TW), :].astype(F32) * m).astype(BF16)
        bm[i] = tile
        bt[i] = tile.T

    for name in ("o", "v"):

        @pl.loop(1, plane[name])
        def _(k):
            plane_copy(name, k, True).wait_recv()

    def along_z(k):
        return lax.rem(z + k + d.Z, d.Z) * 2 + c, b

    def along_y(k):
        return g, lax.rem(y + k + d.Y, d.Y) * d.X + x

    def pos_z(k):
        return lax.rem(z + k + d.Z, d.Z)

    def pos_y(k):
        return lax.rem(y + k + d.Y, d.Y)

    def last_block(name, off, sub, core):
        if name == "o":
            h = d.Y // nsub
            return go.at[pos_z(off), core, pl.ds(sub * h, h)]
        h = d.Z // nsub
        return gv.at[pl.ds(sub * h, h), core, pos_y(off)]

    last_axis = {"o": along_z, "v": along_y}

    def run(stage, sizes, axis, block, nsubs, forward):
        plans = {name: ring_plan(sizes[name], nsubs) for name in ("o", "v")}

        def send(name, e):
            dirn, k, sub = e
            ref = block(name, -dirn * (k - 1), sub)
            i = t[stage + name][e]
            cp = rcopy(ref, ref, i, i, *axis[name](dirn))
            cp.start()
            sends.append(cp)

        for name in ("o", "v"):
            for e in plans[name]:
                if e[1] == 1:
                    send(name, e)
        if forward:
            for name in ("o", "v"):
                forward(name, None)
        order = []
        for n in range(max(len(plans["o"]), len(plans["v"]))):
            for name in ("v", "o"):
                if n < len(plans[name]):
                    order.append((name, plans[name][n]))
        for name, e in order:
            dirn, k, sub = e
            ref = block(name, -dirn * k, sub)
            i = t[stage + name][e]
            rcopy(ref, ref, i, i, g, b).wait_recv()
            nxt = (dirn, k + 1, sub)
            if nxt in plans[name]:
                send(name, nxt)
            if forward:
                forward(name, e)

    def sibling(name, e):
        if e is None:
            ref = go.at[z, c] if name == "o" else gv.at[:, c, y]
            i = t["own" + name]
        else:
            dirn, k, sub = e
            ref = last_block(name, -dirn * k, sub, c)
            i = t["sib" + name][e]
        cp = rcopy(ref, ref, i, i, sib, b)
        cp.start()
        sends.append(cp)

    def from_sibling(name):
        ref = go.at[z, 1 - c] if name == "o" else gv.at[:, 1 - c, y]
        i = t["own" + name]
        rcopy(ref, ref, i, i, g, b).wait_recv()
        n = d.Z if name == "o" else d.Y
        for e in ring_plan(n, nsub):
            dirn, k, sub = e
            ref = last_block(name, -dirn * k, sub, 1 - c)
            i = t["sib" + name][e]
            rcopy(ref, ref, i, i, g, b).wait_recv()

    run(
        "last",
        {"o": d.Z, "v": d.Y},
        last_axis,
        lambda name, off, sub: last_block(name, off, sub, c),
        nsub,
        sibling,
    )
    from_sibling("v")

    def tiles_of(ref, i):
        return ref[i // 2, lax.rem(i, 2)].reshape(d.K, TW, TW)

    @pl.loop(0, d.NT, unroll=2)
    def _(kk):
        j = lax.rem(b // d.HP + kk, d.NT)
        row = owner_ref[j]
        tiles = tiles_of(gv, row)
        left = jnp.concatenate([tiles[s] for s in range(d.K)], axis=1)
        right = jnp.concatenate(
            [bm[lax.rem(row + voff_ref[s], d.NT)] for s in range(d.K)], axis=0
        )
        value = jnp.dot(left, right, preferred_element_type=F32).astype(BF16)
        for h in range(d.HP):
            to = j * d.HP + h
            rbuf[to] = value[h * d.CH : (h + 1) * d.CH]

            @pl.when(to != b)
            def _():
                rcopy(rbuf.at[to], rb.at[b], t["R"] + to, t["R"] + b, g, to).start()

            @pl.when(to == b)
            def _():
                rb[b] = value[h * d.CH : (h + 1) * d.CH]

    from_sibling("o")

    @pl.loop(0, d.NT, unroll=2)
    def _(kk):
        j = lax.rem(g + kk + b // d.HP, d.NT)
        col = owner_ref[j]
        lefts, rights = [], []
        for s in range(d.K):
            i = lax.rem(col - ooff_ref[s] + d.NT, d.NT)
            lefts.append(bt[i])
            rows = go[i // 2, lax.rem(i, 2)].reshape(d.K, TW, TW)[s]
            rights.append(rows)
        value = jnp.dot(
            jnp.concatenate(lefts, axis=1),
            jnp.concatenate(rights, axis=0),
            preferred_element_type=F32,
        ).astype(BF16)
        lbuf[j] = value

        @pl.when(j != g)
        def _():
            rcopy(lbuf.at[j], lg.at[g], t["Lg"] + j, t["Lg"] + g, j, b).start()

        @pl.when(j == g)
        def _():
            lg[g] = value

    @pl.loop(0, d.NT)
    def _(kk):
        j = lax.rem(g - kk - b // d.HP + 2 * d.NT, d.NT)

        @pl.when(j != g)
        def _():
            rcopy(lg.at[j], lg.at[j], t["Lg"] + j, t["Lg"] + j, j, b).wait_recv()

        for h in range(d.HP):
            to = j * d.HP + h
            src = lg.at[j, pl.ds(h * d.CH, d.CH)]

            @pl.when(to != b)
            def _():
                rcopy(src, lb.at[b], t["Lb"] + to, t["Lb"] + b, g, to).start()

            @pl.when(to == b)
            def _():
                lb[b] = src[...]

    for name in ("o", "v"):

        @pl.loop(1, plane[name])
        def _(k):
            plane_copy(name, k, False).wait_send()

    for cp in sends:
        cp.wait_send()

    @pl.loop(1, d.NB)
    def _(k):
        q = lax.rem(b + k, d.NB)
        rcopy(rb.at[q], rb.at[q], t["R"] + q, t["R"] + q, g, q).wait()

    @pl.loop(1, d.NG)
    def _(k):
        q = lax.rem(g + k, d.NG)
        rcopy(lbuf.at[q], lbuf.at[q], t["Lg"] + q, t["Lg"] + q, q, b).wait_send()

    @pl.loop(1, d.NB)
    def _(k):
        q = lax.rem(b + k, d.NB)
        rcopy(lb.at[q], lb.at[q], t["Lb"] + q, t["Lb"] + q, g, q).wait()

    n16 = d.NB * 16
    prod = jnp.zeros((n16, n16), F32)
    for r in range(d.CH // 16):
        left = lb[:, 16 * r : 16 * r + 16, :].reshape(n16, TW)
        right = rb[:, 16 * r : 16 * r + 16, :].reshape(n16, TW)
        prod = prod + lax.dot_general(
            left, right, (((1,), (1,)), ((), ())), preferred_element_type=F32
        )
    ii = lax.broadcasted_iota(jnp.int32, (n16, n16), 0)
    jj = lax.broadcasted_iota(jnp.int32, (n16, n16), 1)
    prod = jnp.where((ii & 15) == (jj & 15), prod, 0.0)
    folded = jnp.sum(prod.reshape(d.NB, 16, n16), axis=1)
    pick = (
        lax.broadcasted_iota(jnp.int32, (n16, TW), 0) // 16
        == lax.broadcasted_iota(jnp.int32, (n16, TW), 1)
    ).astype(F32)
    part = jnp.dot(
        folded, pick, precision=lax.Precision.HIGHEST, preferred_element_type=F32
    )
    for p in range(d.NB):
        s1[p] = part[p : p + 1]
    s1r[b] = s1[b]

    @pl.loop(1, d.NB)
    def _(k):
        q = lax.rem(b + k, d.NB)
        rcopy(s1.at[q], s1r.at[b], t["S1"] + q, t["S1"] + b, g, q).start()

    @pl.loop(1, d.NB)
    def _(k):
        q = lax.rem(b + k, d.NB)
        rcopy(s1r.at[q], s1r.at[q], t["S1"] + q, t["S1"] + q, g, q).wait_recv()

    s2[g] = jnp.sum(s1r[...], axis=0)

    @pl.loop(1, d.NG)
    def _(k):
        q = lax.rem(g + k, d.NG)
        rcopy(s2.at[g], s2.at[g], t["S2"] + q, t["S2"] + g, q, b).start()

    @pl.loop(1, d.NB)
    def _(k):
        q = lax.rem(b + k, d.NB)
        rcopy(s1.at[q], s1.at[q], t["S1"] + q, t["S1"] + q, g, q).wait_send()

    @pl.loop(1, d.NG)
    def _(k):
        q = lax.rem(g + k, d.NG)
        rcopy(s2.at[q], s2.at[q], t["S2"] + q, t["S2"] + q, q, b).wait()

    total = jnp.sum(s2[...], axis=0)
    out_ref[...] = total[:, : d.NB] * (1.0 / (d.NT * TW))


def make(d, nsub):
    t, nsem = layout(d, nsub)

    def body(integrals, mask, owner, otiles, ooff, vtiles, voff):
        vmem = pl.BlockSpec(memory_space=pltpu.VMEM)
        hbm = pl.BlockSpec(memory_space=pltpu.HBM)
        gshape = (d.Z, 2, d.Y, d.X, d.RPD, TW)
        return pl.pallas_call(
            functools.partial(kernel, d, nsub, t),
            out_shape=jax.ShapeDtypeStruct((1, d.NB), F32),
            in_specs=[hbm] * 7,
            out_specs=vmem,
            scratch_shapes=[
                pltpu.SMEM((d.NT, d.NT), jnp.int32),
                pltpu.SMEM((d.NT,), jnp.int32),
                pltpu.SMEM((d.K,), jnp.int32),
                pltpu.SMEM((d.K,), jnp.int32),
                pltpu.VMEM((1, d.NT * TW, TW), BF16),
                pltpu.VMEM(gshape, BF16),
                pltpu.VMEM(gshape, BF16),
                pltpu.VMEM((d.NT, TW, TW), BF16),
                pltpu.VMEM((d.NT, TW, TW), BF16),
                pltpu.VMEM((d.NB, d.CH, TW), BF16),
                pltpu.VMEM((d.NB, d.CH, TW), BF16),
                pltpu.VMEM((d.NT, TW, TW), BF16),
                pltpu.VMEM((d.NT, TW, TW), BF16),
                pltpu.VMEM((d.NB, d.CH, TW), BF16),
                pltpu.VMEM((d.NB, 1, TW), F32),
                pltpu.VMEM((d.NB, 1, TW), F32),
                pltpu.VMEM((d.NG, 1, TW), F32),
                pltpu.SemaphoreType.DMA((nsem,)),
                pltpu.SemaphoreType.DMA((nsem,)),
            ],
            compiler_params=pltpu.CompilerParams(
                collective_id=0, has_side_effects=True, vmem_limit_bytes=60 << 20
            ),
        )(mask, owner, ooff, voff, integrals, otiles, vtiles)

    return body


def solution(mesh, x=4, kcount=8, nsub=2):
    d = Dims(mesh.shape["grp"], mesh.shape["blk"], x, kcount)
    in_specs = (
        P("blk", None, "grp"),
        P(),
        P(),
        P(("grp", "blk"), None),
        P(),
        P(("grp", "blk"), None),
        P(),
    )
    return jax.shard_map(
        make(d, nsub), mesh=mesh, in_specs=in_specs, out_specs=P("blk", None), check_vma=False
    )
```

```python
import functools

import jax
import jax.numpy as jnp
from jax import lax
from jax.experimental import pallas as pl
from jax.experimental.pallas import tpu as pltpu
from jax.sharding import PartitionSpec as P

MESH = pl.DeviceIdType.MESH
SCHEDULE = (("L", 0, 16), ("R", 0, 16))
TW = 128
F32 = jnp.float32
BF16 = jnp.bfloat16


class Dims:
    def __init__(self, ng, nb, x, kcount):
        self.C = 2
        self.NG, self.NB = ng, nb
        self.Z, self.X, self.Y = ng // 2, x, nb // x
        self.NT, self.K = ng, kcount
        self.RPD = kcount * TW // nb
        self.CH = ng * TW // nb
        self.HP = TW // self.CH


def ring_plan(n, nsub):
    plan = []
    for k in range(1, n // 2 + 1):
        for sub in range(nsub):
            last = 2 * k == n
            if not last:
                plan += [(1, k, sub), (-1, k, sub)]
            else:
                plan.append((1 if sub < (nsub + 1) // 2 else -1, k, sub))
    return plan


class Sems:
    def __init__(self):
        self.count = 0

    def take(self, n=1):
        base = self.count
        self.count += n
        return base


def layout(d, nsub):
    s = Sems()
    t = {}
    last = {"o": d.Z, "v": d.Y}
    for name in ("o", "v"):
        t["last" + name] = {e: s.take() for e in ring_plan(last[name], nsub)}
        for stage in ("P", "ring", "sib"):
            t[stage + name] = s.take()
    for name in ("R", "Lb", "S1", "S2"):
        t[name] = s.take()
    t["in"] = s.take(7)
    return t, s.count


def kernel(
    d,
    nsub,
    t,
    mask_hbm,
    owner_hbm,
    ooff_hbm,
    voff_hbm,
    b_hbm,
    ot_ref,
    vt_ref,
    out_ref,
    mask_ref,
    owner_ref,
    ooff_ref,
    voff_ref,
    b_ref,
    go,
    gv,
    bm,
    bt,
    rbuf,
    rb,
    lbuf,
    lb,
    s1,
    s1r,
    s2,
    ssem,
    rsem,
):
    g = lax.axis_index("grp")
    b = lax.axis_index("blk")
    z, c = g // 2, lax.rem(g, 2)
    y, x = b // d.X, lax.rem(b, d.X)
    sib = z * 2 + (1 - c)

    def rcopy(src, dst, i, j, gg, bb):
        return pltpu.make_async_remote_copy(
            src_ref=src,
            dst_ref=dst,
            send_sem=ssem.at[i],
            recv_sem=rsem.at[j],
            device_id=(gg, bb),
            device_id_type=MESH,
        )

    loads = [
        pltpu.make_async_copy(src, dst, ssem.at[t["in"] + i])
        for i, (src, dst) in enumerate(
            [
                (mask_hbm, mask_ref),
                (owner_hbm, owner_ref),
                (ooff_hbm, ooff_ref),
                (voff_hbm, voff_ref),
                (b_hbm, b_ref),
            ]
        )
    ]
    for cp in loads:
        cp.start()
    pltpu.make_async_copy(ot_ref, go.at[z, c, y, x], rsem.at[t["Po"]]).start()
    pltpu.make_async_copy(vt_ref, gv.at[z, c, y, x], rsem.at[t["Pv"]]).start()

    barrier = pltpu.get_barrier_semaphore()

    def signal(gg, bb):
        pl.semaphore_signal(barrier, inc=1, device_id=(gg, bb), device_id_type=MESH)

    @pl.loop(1, d.NG)
    def _(k):
        signal(lax.rem(g + k, d.NG), b)

    @pl.loop(1, d.NB)
    def _(k):
        signal(g, lax.rem(b + k, d.NB))

    for dx in range(1, d.X):

        @pl.loop(1, d.Z)
        def _(k):
            signal(lax.rem(z + k, d.Z) * 2 + c, y * d.X + lax.rem(x + dx, d.X))

    source = lax.rem((g + d.NG - b // d.HP) * 7, d.NG)

    @pl.loop(0, d.NB)
    def _(k):
        @pl.when((source != g) | (k != b))
        def _():
            signal(source, k)

    others = d.NG + d.NB - 2 + (d.X - 1) * (d.Z - 1) + d.NB
    pl.semaphore_wait(barrier, others - (source == g).astype(jnp.int32))

    bufs = {"o": go, "v": gv}

    def plane_copy(name, k):
        xx = lax.rem(x + lax.rem(k, d.X), d.X)
        if name == "o":
            ref, src = go.at[z, c, y, x], ot_ref
            to = (g, lax.rem(y + k // d.X, d.Y) * d.X + xx)
        else:
            ref, src = gv.at[z, c, y, x], vt_ref
            to = (lax.rem(z + k // d.X, d.Z) * 2 + c, y * d.X + xx)
        i = t["P" + name]
        return rcopy(src, ref, i, i, *to)

    def plane_bytes(name):
        n = plane[name] - 1
        ref = rbuf.reshape(d.NB * d.CH, TW).at[pl.ds(0, n * d.RPD)]
        i = t["P" + name]
        return rcopy(ref, ref, i, i, g, b)

    plane = {"o": d.Y * d.X, "v": d.Z * d.X}
    for name in ("o", "v"):

        @pl.loop(1, plane[name])
        def _(k):
            plane_copy(name, k).start()

    for cp in loads:
        cp.wait()

    own = owner_ref[g]

    @pl.loop(0, d.NT)
    def _(i):
        m = mask_ref[i, own].astype(F32)
        tile = (b_ref[0, pl.ds(pl.multiple_of(i * TW, TW), TW), :].astype(F32) * m).astype(BF16)
        bm[i] = tile
        bt[i] = tile.T

    for name in ("o", "v"):
        ref = go.at[z, c] if name == "o" else gv.at[:, c, y]
        rcopy(ref, ref, t["P" + name], t["P" + name], g, b).wait_recv()

    def along_z(k):
        return lax.rem(z + k + d.Z, d.Z) * 2 + c, b

    def along_y(k):
        return g, lax.rem(y + k + d.Y, d.Y) * d.X + x

    def pos_z(k):
        return lax.rem(z + k + d.Z, d.Z)

    def pos_y(k):
        return lax.rem(y + k + d.Y, d.Y)

    def last_block(name, off, sub, core):
        if name == "o":
            h = d.Y // nsub
            return go.at[pos_z(off), core, pl.ds(sub * h, h)]
        h = d.Z // nsub
        return gv.at[pl.ds(sub * h, h), core, pos_y(off)]

    last_axis = {"o": along_z, "v": along_y}

    def run(stage, sizes, axis, block, nsubs, forward):
        plans = {name: ring_plan(sizes[name], nsubs) for name in ("o", "v")}

        def send(name, e):
            dirn, k, sub = e
            ref = block(name, -dirn * (k - 1), sub)
            rcopy(ref, ref, t["ring" + name], t[stage + name][e], *axis[name](dirn)).start()

        for name in ("o", "v"):
            for e in plans[name]:
                if e[1] == 1:
                    send(name, e)
        if forward:
            for name in ("o", "v"):
                forward(name, None)
        order = []
        for n in range(max(len(plans["o"]), len(plans["v"]))):
            for name in ("v", "o"):
                if n < len(plans[name]):
                    order.append((name, plans[name][n]))
        for name, e in order:
            dirn, k, sub = e
            ref = block(name, -dirn * k, sub)
            i = t[stage + name][e]
            rcopy(ref, ref, i, i, g, b).wait_recv()
            nxt = (dirn, k + 1, sub)
            if nxt in plans[name]:
                send(name, nxt)
            if forward:
                forward(name, e)

    def sibling(name, e):
        if e is None:
            ref = go.at[z, c] if name == "o" else gv.at[:, c, y]
        else:
            dirn, k, sub = e
            ref = last_block(name, -dirn * k, sub, c)
        i = t["sib" + name]
        rcopy(ref, ref, i, i, sib, b).start()

    def from_sibling(name):
        ref = bufs[name].at[:, 1 - c]
        i = t["sib" + name]
        rcopy(ref, ref, i, i, g, b).wait_recv()

    run(
        "last",
        {"o": d.Z, "v": d.Y},
        last_axis,
        lambda name, off, sub: last_block(name, off, sub, c),
        nsub,
        sibling,
    )
    from_sibling("v")
    from_sibling("o")

    def tiles_of(ref, i):
        return ref[i // 2, lax.rem(i, 2)].reshape(d.K, TW, TW)

    def virtual_slot(kk):
        at = lax.rem(b // d.HP + kk, d.NT)
        j = lax.rem((g + d.NG - at) * 7, d.NG)
        row = owner_ref[j]
        tiles = tiles_of(gv, row)
        left = jnp.concatenate([tiles[s] for s in range(d.K)], axis=1)
        right = jnp.concatenate(
            [bm[lax.rem(row + voff_ref[s], d.NT)] for s in range(d.K)], axis=0
        )
        value = jnp.dot(left, right, preferred_element_type=F32).astype(BF16)
        for h in range(d.HP):
            to = at * d.HP + h
            rbuf[to] = value[h * d.CH : (h + 1) * d.CH]

            @pl.when(to != b)
            def _():
                rcopy(rbuf.at[to], rb.at[b], t["R"], t["R"], g, to).start()

            @pl.when(to == b)
            def _():
                rb[b] = value[h * d.CH : (h + 1) * d.CH]

    def occupied_slot(kk):
        at = lax.rem(b // d.HP + kk, d.NT)
        j = lax.rem(at + 7 * g, d.NG)
        col = owner_ref[j]
        lefts, rights = [], []
        for s in range(d.K):
            i = lax.rem(col - ooff_ref[s] + d.NT, d.NT)
            lefts.append(bt[i])
            rows = go[i // 2, lax.rem(i, 2)].reshape(d.K, TW, TW)[s]
            rights.append(rows)
        value = jnp.dot(
            jnp.concatenate(lefts, axis=1),
            jnp.concatenate(rights, axis=0),
            preferred_element_type=F32,
        ).astype(BF16)
        lbuf[j] = value

        for h in range(d.HP):
            to = at * d.HP + h
            src = lbuf.at[j, pl.ds(h * d.CH, d.CH)]

            @pl.when((to != b) | (j != g))
            def _():
                rcopy(src, lb.at[b], t["Lb"], t["Lb"], j, to).start()

            @pl.when((to == b) & (j == g))
            def _():
                lb[b] = value[h * d.CH : (h + 1) * d.CH]

    steps = {"L": occupied_slot, "R": virtual_slot}
    for what, lo, hi in SCHEDULE:

        @pl.loop(lo * d.NT // 16, hi * d.NT // 16, unroll=2)
        def _(kk):
            steps[what](kk)

    for name in ("o", "v"):
        plane_bytes(name).wait_send()
        ref = bufs[name].at[:, c]
        rcopy(ref, ref, t["sib" + name], t["sib" + name], g, b).wait_send()
        ref = bufs[name].at[pl.ds(0, d.Z - 1), c] if name == "o" else bufs[name].at[:, c, pl.ds(0, d.Y - 1)]
        rcopy(ref, ref, t["ring" + name], t["ring" + name], g, b).wait_send()

    def wait_all(ref, n, name):
        part = ref.at[pl.ds(0, n)]
        cp = rcopy(part, part, t[name], t[name], g, b)
        cp.wait_send()
        cp.wait_recv()

    wait_all(rb, d.NB - 1, "R")

    @pl.when(source != g)
    def _():
        wait_all(lb, d.NB, "Lb")

    @pl.when(source == g)
    def _():
        wait_all(lb, d.NB - 1, "Lb")

    n16 = d.NB * 16
    prod = jnp.zeros((n16, n16), F32)
    for r in range(d.CH // 16):
        left = lb[:, 16 * r : 16 * r + 16, :].reshape(n16, TW)
        right = rb[:, 16 * r : 16 * r + 16, :].reshape(n16, TW)
        prod = prod + lax.dot_general(
            left, right, (((1,), (1,)), ((), ())), preferred_element_type=F32
        )
    ii = lax.broadcasted_iota(jnp.int32, (n16, n16), 0)
    jj = lax.broadcasted_iota(jnp.int32, (n16, n16), 1)
    prod = jnp.where((ii & 15) == (jj & 15), prod, 0.0)
    folded = jnp.sum(prod.reshape(d.NB, 16, n16), axis=1)
    pick = (
        lax.broadcasted_iota(jnp.int32, (n16, TW), 0) // 16
        == lax.broadcasted_iota(jnp.int32, (n16, TW), 1)
    ).astype(F32)
    part = jnp.dot(
        folded, pick, precision=lax.Precision.HIGHEST, preferred_element_type=F32
    )
    for p in range(d.NB):
        s1[p] = part[p : p + 1]
    s1r[b] = s1[b]

    @pl.loop(1, d.NB)
    def _(k):
        q = lax.rem(b + k, d.NB)
        rcopy(s1.at[q], s1r.at[b], t["S1"], t["S1"], g, q).start()

    wait_all(s1r, d.NB - 1, "S1")
    s2[g] = jnp.sum(s1r[...], axis=0)

    @pl.loop(1, d.NG)
    def _(k):
        q = lax.rem(g + k, d.NG)
        rcopy(s2.at[g], s2.at[g], t["S2"], t["S2"], q, b).start()

    wait_all(s2, d.NG - 1, "S2")
    total = jnp.sum(s2[...], axis=0)
    out_ref[...] = total[:, : d.NB] * (1.0 / (d.NT * TW))


def make(d, nsub):
    t, nsem = layout(d, nsub)

    def body(integrals, mask, owner, otiles, ooff, vtiles, voff):
        vmem = pl.BlockSpec(memory_space=pltpu.VMEM)
        hbm = pl.BlockSpec(memory_space=pltpu.HBM)
        gshape = (d.Z, 2, d.Y, d.X, d.RPD, TW)
        return pl.pallas_call(
            functools.partial(kernel, d, nsub, t),
            out_shape=jax.ShapeDtypeStruct((1, d.NB), F32),
            in_specs=[hbm] * 7,
            out_specs=vmem,
            scratch_shapes=[
                pltpu.SMEM((d.NT, d.NT), jnp.int32),
                pltpu.SMEM((d.NT,), jnp.int32),
                pltpu.SMEM((d.K,), jnp.int32),
                pltpu.SMEM((d.K,), jnp.int32),
                pltpu.VMEM((1, d.NT * TW, TW), BF16),
                pltpu.VMEM(gshape, BF16),
                pltpu.VMEM(gshape, BF16),
                pltpu.VMEM((d.NT, TW, TW), BF16),
                pltpu.VMEM((d.NT, TW, TW), BF16),
                pltpu.VMEM((d.NB, d.CH, TW), BF16),
                pltpu.VMEM((d.NB, d.CH, TW), BF16),
                pltpu.VMEM((d.NT, TW, TW), BF16),
                pltpu.VMEM((d.NB, d.CH, TW), BF16),
                pltpu.VMEM((d.NB, 1, TW), F32),
                pltpu.VMEM((d.NB, 1, TW), F32),
                pltpu.VMEM((d.NG, 1, TW), F32),
                pltpu.SemaphoreType.DMA((nsem,)),
                pltpu.SemaphoreType.DMA((nsem,)),
            ],
            compiler_params=pltpu.CompilerParams(
                collective_id=0, has_side_effects=True, vmem_limit_bytes=60 << 20
            ),
        )(mask, owner, ooff, voff, integrals, otiles, vtiles)

    return body


def solution(mesh, x=4, kcount=8, nsub=2):
    d = Dims(mesh.shape["grp"], mesh.shape["blk"], x, kcount)
    in_specs = (
        P("blk", None, "grp"),
        P(),
        P(),
        P(("grp", "blk"), None),
        P(),
        P(("grp", "blk"), None),
        P(),
    )
    return jax.shard_map(
        make(d, nsub), mesh=mesh, in_specs=in_specs, out_specs=P("blk", None), check_vma=False
    )
```

```python
import functools

import jax
import jax.numpy as jnp
from jax import lax
from jax.experimental import pallas as pl
from jax.experimental.pallas import tpu as pltpu
from jax.sharding import PartitionSpec as P

MESH = pl.DeviceIdType.MESH
SCHEDULE = (("L", 0, 16), ("R", 0, 16))
TW = 128
F32 = jnp.float32
BF16 = jnp.bfloat16


class Dims:
    def __init__(self, ng, nb, x, kcount):
        self.C = 2
        self.NG, self.NB = ng, nb
        self.Z, self.X, self.Y = ng // 2, x, nb // x
        self.NT, self.K = ng, kcount
        self.RPD = kcount * TW // nb
        self.CH = ng * TW // nb
        self.HP = TW // self.CH


def ring_plan(n, nsub):
    plan = []
    for k in range(1, n // 2 + 1):
        for sub in range(nsub):
            last = 2 * k == n
            if not last:
                plan += [(1, k, sub), (-1, k, sub)]
            else:
                plan.append((1 if sub < (nsub + 1) // 2 else -1, k, sub))
    return plan


class Sems:
    def __init__(self):
        self.count = 0

    def take(self, n=1):
        base = self.count
        self.count += n
        return base


def layout(d, nsub):
    s = Sems()
    t = {}
    last = {"o": d.Z, "v": d.Y}
    for name in ("o", "v"):
        t["last" + name] = {e: s.take() for e in ring_plan(last[name], nsub)}
        for stage in ("P", "ring", "sib"):
            t[stage + name] = s.take()
    for name in ("R", "Lb", "S1", "S2"):
        t[name] = s.take()
    t["in"] = s.take(7)
    return t, s.count


def kernel(
    d,
    nsub,
    t,
    mask_hbm,
    owner_hbm,
    ooff_hbm,
    voff_hbm,
    b_hbm,
    ot_ref,
    vt_ref,
    out_ref,
    mask_ref,
    owner_ref,
    ooff_ref,
    voff_ref,
    b_ref,
    go,
    gv,
    bm,
    bt,
    rbuf,
    rb,
    lbuf,
    lb,
    s1,
    s1r,
    s2,
    ssem,
    rsem,
):
    g = lax.axis_index("grp")
    b = lax.axis_index("blk")
    z, c = g // 2, lax.rem(g, 2)
    y, x = b // d.X, lax.rem(b, d.X)
    sib = z * 2 + (1 - c)

    def rcopy(src, dst, i, j, gg, bb):
        return pltpu.make_async_remote_copy(
            src_ref=src,
            dst_ref=dst,
            send_sem=ssem.at[i],
            recv_sem=rsem.at[j],
            device_id=(gg, bb),
            device_id_type=MESH,
        )

    loads = [
        pltpu.make_async_copy(src, dst, ssem.at[t["in"] + i])
        for i, (src, dst) in enumerate(
            [
                (mask_hbm, mask_ref),
                (owner_hbm, owner_ref),
                (ooff_hbm, ooff_ref),
                (voff_hbm, voff_ref),
                (b_hbm, b_ref),
            ]
        )
    ]
    for cp in loads:
        cp.start()
    pltpu.make_async_copy(ot_ref, go.at[z, c, y, x], rsem.at[t["Po"]]).start()
    pltpu.make_async_copy(vt_ref, gv.at[z, c, y, x], rsem.at[t["Pv"]]).start()

    barrier = pltpu.get_barrier_semaphore()

    def signal(gg, bb):
        pl.semaphore_signal(barrier, inc=1, device_id=(gg, bb), device_id_type=MESH)

    @pl.loop(1, d.NG, unroll=d.NG - 1)
    def _(k):
        signal(lax.rem(g + k, d.NG), b)

    @pl.loop(1, d.NB, unroll=d.NB - 1)
    def _(k):
        signal(g, lax.rem(b + k, d.NB))

    for dx in range(1, d.X):

        @pl.loop(1, d.Z, unroll=d.Z - 1)
        def _(k):
            signal(lax.rem(z + k, d.Z) * 2 + c, y * d.X + lax.rem(x + dx, d.X))

    source = lax.rem((g + d.NG - b // d.HP) * 7, d.NG)

    @pl.loop(0, d.NB)
    def _(k):
        @pl.when((source != g) | (k != b))
        def _():
            signal(source, k)

    others = d.NG + d.NB - 2 + (d.X - 1) * (d.Z - 1) + d.NB
    pl.semaphore_wait(barrier, others - (source == g).astype(jnp.int32))

    bufs = {"o": go, "v": gv}

    def plane_copy(name, k):
        xx = lax.rem(x + lax.rem(k, d.X), d.X)
        if name == "o":
            ref, src = go.at[z, c, y, x], ot_ref
            to = (g, lax.rem(y + k // d.X, d.Y) * d.X + xx)
        else:
            ref, src = gv.at[z, c, y, x], vt_ref
            to = (lax.rem(z + k // d.X, d.Z) * 2 + c, y * d.X + xx)
        i = t["P" + name]
        return rcopy(src, ref, i, i, *to)

    def plane_bytes(name):
        n = plane[name] - 1
        ref = rbuf.reshape(d.NB * d.CH, TW).at[pl.ds(0, n * d.RPD)]
        i = t["P" + name]
        return rcopy(ref, ref, i, i, g, b)

    plane = {"o": d.Y * d.X, "v": d.Z * d.X}

    @pl.loop(1, min(plane.values()))
    def _(k):
        for name in ("o", "v"):
            plane_copy(name, k).start()

    for name in ("o", "v"):
        if plane[name] > min(plane.values()):

            @pl.loop(min(plane.values()), plane[name])
            def _(k):
                plane_copy(name, k).start()

    for cp in loads:
        cp.wait()

    own = owner_ref[g]

    @pl.loop(0, d.NT)
    def _(i):
        m = mask_ref[i, own].astype(F32)
        tile = (b_ref[0, pl.ds(pl.multiple_of(i * TW, TW), TW), :].astype(F32) * m).astype(BF16)
        bm[i] = tile
        bt[i] = tile.T

    def plane_arrived(name):
        ref = go.at[z, c] if name == "o" else gv.at[:, c, y]
        rcopy(ref, ref, t["P" + name], t["P" + name], g, b).wait_recv()

    def along_z(k):
        return lax.rem(z + k + d.Z, d.Z) * 2 + c, b

    def along_y(k):
        return g, lax.rem(y + k + d.Y, d.Y) * d.X + x

    def pos_z(k):
        return lax.rem(z + k + d.Z, d.Z)

    def pos_y(k):
        return lax.rem(y + k + d.Y, d.Y)

    def last_block(name, off, sub, core):
        if name == "o":
            h = d.Y // nsub
            return go.at[pos_z(off), core, pl.ds(sub * h, h)]
        h = d.Z // nsub
        return gv.at[pl.ds(sub * h, h), core, pos_y(off)]

    last_axis = {"o": along_z, "v": along_y}

    def run(stage, sizes, axis, block, nsubs, forward):
        plans = {name: ring_plan(sizes[name], nsubs) for name in ("o", "v")}

        def send(name, e):
            dirn, k, sub = e
            ref = block(name, -dirn * (k - 1), sub)
            rcopy(ref, ref, t["ring" + name], t[stage + name][e], *axis[name](dirn)).start()

        for name in ("o", "v"):
            plane_arrived(name)
            for e in plans[name]:
                if e[1] == 1:
                    send(name, e)
        if forward:
            for name in ("o", "v"):
                forward(name, None)
        order = []
        for n in range(max(len(plans["o"]), len(plans["v"]))):
            for name in ("v", "o"):
                if n < len(plans[name]):
                    order.append((name, plans[name][n]))
        for name, e in order:
            dirn, k, sub = e
            ref = block(name, -dirn * k, sub)
            i = t[stage + name][e]
            rcopy(ref, ref, i, i, g, b).wait_recv()
            nxt = (dirn, k + 1, sub)
            if nxt in plans[name]:
                send(name, nxt)
            if forward:
                forward(name, e)

    def sibling(name, e):
        if e is None:
            ref = go.at[z, c] if name == "o" else gv.at[:, c, y]
        else:
            dirn, k, sub = e
            ref = last_block(name, -dirn * k, sub, c)
        i = t["sib" + name]
        rcopy(ref, ref, i, i, sib, b).start()

    def from_sibling(name):
        ref = bufs[name].at[:, 1 - c]
        i = t["sib" + name]
        rcopy(ref, ref, i, i, g, b).wait_recv()

    run(
        "last",
        {"o": d.Z, "v": d.Y},
        last_axis,
        lambda name, off, sub: last_block(name, off, sub, c),
        nsub,
        sibling,
    )
    from_sibling("o")

    def tiles_of(ref, i):
        return ref[i // 2, lax.rem(i, 2)].reshape(d.K, TW, TW)

    def virtual_slot(kk):
        at = lax.rem(b // d.HP + kk, d.NT)
        j = lax.rem((g + d.NG - at) * 7, d.NG)
        row = owner_ref[j]
        tiles = tiles_of(gv, row)
        left = jnp.concatenate([tiles[s] for s in range(d.K)], axis=1)
        right = jnp.concatenate(
            [bm[lax.rem(row + voff_ref[s], d.NT)] for s in range(d.K)], axis=0
        )
        value = jnp.dot(left, right, preferred_element_type=F32).astype(BF16)
        for h in range(d.HP):
            to = at * d.HP + h
            rbuf[to] = value[h * d.CH : (h + 1) * d.CH]

            @pl.when(to != b)
            def _():
                rcopy(rbuf.at[to], rb.at[b], t["R"], t["R"], g, to).start()

            @pl.when(to == b)
            def _():
                rb[b] = value[h * d.CH : (h + 1) * d.CH]

    def occupied_slot(kk):
        at = lax.rem(b // d.HP + kk, d.NT)
        j = lax.rem(at + 7 * g, d.NG)
        col = owner_ref[j]
        lefts, rights = [], []
        for s in range(d.K):
            i = lax.rem(col - ooff_ref[s] + d.NT, d.NT)
            lefts.append(bt[i])
            rows = go[i // 2, lax.rem(i, 2)].reshape(d.K, TW, TW)[s]
            rights.append(rows)
        value = jnp.dot(
            jnp.concatenate(lefts, axis=1),
            jnp.concatenate(rights, axis=0),
            preferred_element_type=F32,
        ).astype(BF16)
        lbuf[j] = value

        for h in range(d.HP):
            to = at * d.HP + h
            src = lbuf.at[j, pl.ds(h * d.CH, d.CH)]

            @pl.when((to != b) | (j != g))
            def _():
                rcopy(src, lb.at[b], t["Lb"], t["Lb"], j, to).start()

            @pl.when((to == b) & (j == g))
            def _():
                lb[b] = value[h * d.CH : (h + 1) * d.CH]

    steps = {"L": occupied_slot, "R": virtual_slot}
    for what, lo, hi in SCHEDULE:
        if what == "R":
            from_sibling("v")

        @pl.loop(lo * d.NT // 16, hi * d.NT // 16, unroll=2)
        def _(kk):
            steps[what](kk)

    for name in ("o", "v"):
        plane_bytes(name).wait_send()
        ref = bufs[name].at[:, c]
        rcopy(ref, ref, t["sib" + name], t["sib" + name], g, b).wait_send()
        ref = bufs[name].at[pl.ds(0, d.Z - 1), c] if name == "o" else bufs[name].at[:, c, pl.ds(0, d.Y - 1)]
        rcopy(ref, ref, t["ring" + name], t["ring" + name], g, b).wait_send()

    def wait_all(ref, n, name):
        part = ref.at[pl.ds(0, n)]
        cp = rcopy(part, part, t[name], t[name], g, b)
        cp.wait_send()
        cp.wait_recv()

    wait_all(rb, d.NB - 1, "R")

    @pl.when(source != g)
    def _():
        wait_all(lb, d.NB, "Lb")

    @pl.when(source == g)
    def _():
        wait_all(lb, d.NB - 1, "Lb")

    n16 = d.NB * 16
    prod = jnp.zeros((n16, n16), F32)
    for r in range(d.CH // 16):
        left = lb[:, 16 * r : 16 * r + 16, :].reshape(n16, TW)
        right = rb[:, 16 * r : 16 * r + 16, :].reshape(n16, TW)
        prod = prod + lax.dot_general(
            left, right, (((1,), (1,)), ((), ())), preferred_element_type=F32
        )
    ii = lax.broadcasted_iota(jnp.int32, (n16, n16), 0)
    jj = lax.broadcasted_iota(jnp.int32, (n16, n16), 1)
    prod = jnp.where((ii & 15) == (jj & 15), prod, 0.0)
    folded = jnp.sum(prod.reshape(d.NB, 16, n16), axis=1)
    pick = (
        lax.broadcasted_iota(jnp.int32, (n16, TW), 0) // 16
        == lax.broadcasted_iota(jnp.int32, (n16, TW), 1)
    ).astype(F32)
    part = jnp.dot(
        folded, pick, precision=lax.Precision.HIGHEST, preferred_element_type=F32
    )
    for p in range(d.NB):
        s1[p] = part[p : p + 1]
    s1r[b] = s1[b]

    @pl.loop(1, d.NB)
    def _(k):
        q = lax.rem(b + k, d.NB)
        rcopy(s1.at[q], s1r.at[b], t["S1"], t["S1"], g, q).start()

    wait_all(s1r, d.NB - 1, "S1")
    s2[g] = jnp.sum(s1r[...], axis=0)

    @pl.loop(1, d.NG)
    def _(k):
        q = lax.rem(g + k, d.NG)
        rcopy(s2.at[g], s2.at[g], t["S2"], t["S2"], q, b).start()

    wait_all(s2, d.NG - 1, "S2")
    total = jnp.sum(s2[...], axis=0)
    out_ref[...] = total[:, : d.NB] * (1.0 / (d.NT * TW))


def make(d, nsub):
    t, nsem = layout(d, nsub)

    def body(integrals, mask, owner, otiles, ooff, vtiles, voff):
        vmem = pl.BlockSpec(memory_space=pltpu.VMEM)
        hbm = pl.BlockSpec(memory_space=pltpu.HBM)
        gshape = (d.Z, 2, d.Y, d.X, d.RPD, TW)
        return pl.pallas_call(
            functools.partial(kernel, d, nsub, t),
            out_shape=jax.ShapeDtypeStruct((1, d.NB), F32),
            in_specs=[hbm] * 7,
            out_specs=vmem,
            scratch_shapes=[
                pltpu.SMEM((d.NT, d.NT), jnp.int32),
                pltpu.SMEM((d.NT,), jnp.int32),
                pltpu.SMEM((d.K,), jnp.int32),
                pltpu.SMEM((d.K,), jnp.int32),
                pltpu.VMEM((1, d.NT * TW, TW), BF16),
                pltpu.VMEM(gshape, BF16),
                pltpu.VMEM(gshape, BF16),
                pltpu.VMEM((d.NT, TW, TW), BF16),
                pltpu.VMEM((d.NT, TW, TW), BF16),
                pltpu.VMEM((d.NB, d.CH, TW), BF16),
                pltpu.VMEM((d.NB, d.CH, TW), BF16),
                pltpu.VMEM((d.NT, TW, TW), BF16),
                pltpu.VMEM((d.NB, d.CH, TW), BF16),
                pltpu.VMEM((d.NB, 1, TW), F32),
                pltpu.VMEM((d.NB, 1, TW), F32),
                pltpu.VMEM((d.NG, 1, TW), F32),
                pltpu.SemaphoreType.DMA((nsem,)),
                pltpu.SemaphoreType.DMA((nsem,)),
            ],
            compiler_params=pltpu.CompilerParams(
                collective_id=0, has_side_effects=True, vmem_limit_bytes=60 << 20
            ),
        )(mask, owner, ooff, voff, integrals, otiles, vtiles)

    return body


def solution(mesh, x=4, kcount=8, nsub=4):
    d = Dims(mesh.shape["grp"], mesh.shape["blk"], x, kcount)
    in_specs = (
        P("blk", None, "grp"),
        P(),
        P(),
        P(("grp", "blk"), None),
        P(),
        P(("grp", "blk"), None),
        P(),
    )
    return jax.shard_map(
        make(d, nsub), mesh=mesh, in_specs=in_specs, out_specs=P("blk", None), check_vma=False
    )
```

```python
import functools

import jax
import jax.numpy as jnp
from jax import lax
from jax.experimental import pallas as pl
from jax.experimental.pallas import tpu as pltpu
from jax.sharding import PartitionSpec as P

MESH = pl.DeviceIdType.MESH
SCHEDULE = (("L", 0, 16), ("R", 0, 16))
TW = 128
F32 = jnp.float32
BF16 = jnp.bfloat16


class Dims:
    def __init__(self, ng, nb, x, kcount):
        self.C = 2
        self.NG, self.NB = ng, nb
        self.Z, self.X, self.Y = ng // 2, x, nb // x
        self.NT, self.K = ng, kcount
        self.RPD = kcount * TW // nb
        self.CH = ng * TW // nb
        self.HP = TW // self.CH


def ring_plan(n, nsub):
    plan = []
    for k in range(1, n // 2 + 1):
        for sub in range(nsub):
            last = 2 * k == n
            if not last:
                plan += [(1, k, sub), (-1, k, sub)]
            else:
                plan.append((1 if sub < (nsub + 1) // 2 else -1, k, sub))
    return plan


class Sems:
    def __init__(self):
        self.count = 0

    def take(self, n=1):
        base = self.count
        self.count += n
        return base


def layout(d, nsub):
    s = Sems()
    t = {}
    last = {"o": d.Z, "v": d.Y}
    for name in ("o", "v"):
        t["last" + name] = {e: s.take() for e in ring_plan(last[name], nsub)}
        for stage in ("P", "ring", "sib"):
            t[stage + name] = s.take()
    for name in ("R", "Lb", "S1", "S2"):
        t[name] = s.take()
    t["in"] = s.take(7)
    return t, s.count


def kernel(
    d,
    nsub,
    t,
    mask_hbm,
    owner_hbm,
    ooff_hbm,
    voff_hbm,
    b_hbm,
    ot_ref,
    vt_ref,
    out_ref,
    mask_ref,
    owner_ref,
    ooff_ref,
    voff_ref,
    b_ref,
    go,
    gv,
    bm,
    bt,
    rbuf,
    rb,
    lbuf,
    lb,
    s1,
    s1r,
    s2,
    ssem,
    rsem,
):
    g = lax.axis_index("grp")
    b = lax.axis_index("blk")
    z, c = g // 2, lax.rem(g, 2)
    y, x = b // d.X, lax.rem(b, d.X)
    sib = z * 2 + (1 - c)

    def rcopy(src, dst, i, j, gg, bb):
        return pltpu.make_async_remote_copy(
            src_ref=src,
            dst_ref=dst,
            send_sem=ssem.at[i],
            recv_sem=rsem.at[j],
            device_id=(gg, bb),
            device_id_type=MESH,
        )

    loads = [
        pltpu.make_async_copy(src, dst, ssem.at[t["in"] + i])
        for i, (src, dst) in enumerate(
            [
                (mask_hbm, mask_ref),
                (owner_hbm, owner_ref),
                (ooff_hbm, ooff_ref),
                (voff_hbm, voff_ref),
                (b_hbm, b_ref),
            ]
        )
    ]
    for cp in loads:
        cp.start()
    pltpu.make_async_copy(ot_ref, go.at[z, c, y, x], rsem.at[t["Po"]]).start()
    pltpu.make_async_copy(vt_ref, gv.at[z, c, y, x], rsem.at[t["Pv"]]).start()

    barrier = pltpu.get_barrier_semaphore()

    def signal(gg, bb):
        pl.semaphore_signal(barrier, inc=1, device_id=(gg, bb), device_id_type=MESH)

    @pl.loop(1, d.NG, unroll=d.NG - 1)
    def _(k):
        signal(lax.rem(g + k, d.NG), b)

    @pl.loop(1, d.NB, unroll=d.NB - 1)
    def _(k):
        signal(g, lax.rem(b + k, d.NB))

    for dx in range(1, d.X):

        @pl.loop(1, d.Z, unroll=d.Z - 1)
        def _(k):
            signal(lax.rem(z + k, d.Z) * 2 + c, y * d.X + lax.rem(x + dx, d.X))

    source = lax.rem((g + d.NG - b // d.HP) * 7, d.NG)

    @pl.loop(0, d.NB)
    def _(k):
        @pl.when((source != g) | (k != b))
        def _():
            signal(source, k)

    others = d.NG + d.NB - 2 + (d.X - 1) * (d.Z - 1) + d.NB
    pl.semaphore_wait(barrier, others - (source == g).astype(jnp.int32))

    bufs = {"o": go, "v": gv}

    def plane_copy(name, k):
        k = lax.rem(k + plane[name] // 2 - 1, plane[name] - 1) + 1
        xx = lax.rem(x + lax.rem(k, d.X), d.X)
        if name == "o":
            ref, src = go.at[z, c, y, x], ot_ref
            to = (g, lax.rem(y + k // d.X, d.Y) * d.X + xx)
        else:
            ref, src = gv.at[z, c, y, x], vt_ref
            to = (lax.rem(z + k // d.X, d.Z) * 2 + c, y * d.X + xx)
        i = t["P" + name]
        return rcopy(src, ref, i, i, *to)

    def plane_bytes(name):
        n = plane[name] - 1
        ref = rbuf.reshape(d.NB * d.CH, TW).at[pl.ds(0, n * d.RPD)]
        i = t["P" + name]
        return rcopy(ref, ref, i, i, g, b)

    plane = {"o": d.Y * d.X, "v": d.Z * d.X}

    @pl.loop(1, min(plane.values()))
    def _(k):
        for name in ("o", "v"):
            plane_copy(name, k).start()

    for name in ("o", "v"):
        if plane[name] > min(plane.values()):

            @pl.loop(min(plane.values()), plane[name])
            def _(k):
                plane_copy(name, k).start()

    for cp in loads:
        cp.wait()

    own = owner_ref[g]

    @pl.loop(0, d.NT)
    def _(i):
        m = mask_ref[i, own].astype(F32)
        tile = (b_ref[0, pl.ds(pl.multiple_of(i * TW, TW), TW), :].astype(F32) * m).astype(BF16)
        bm[i] = tile
        bt[i] = tile.T

    def plane_arrived(name):
        ref = go.at[z, c] if name == "o" else gv.at[:, c, y]
        rcopy(ref, ref, t["P" + name], t["P" + name], g, b).wait_recv()

    def along_z(k):
        return lax.rem(z + k + d.Z, d.Z) * 2 + c, b

    def along_y(k):
        return g, lax.rem(y + k + d.Y, d.Y) * d.X + x

    def pos_z(k):
        return lax.rem(z + k + d.Z, d.Z)

    def pos_y(k):
        return lax.rem(y + k + d.Y, d.Y)

    def last_block(name, off, sub, core):
        if name == "o":
            h = d.Y // nsub
            return go.at[pos_z(off), core, pl.ds(sub * h, h)]
        h = d.Z // nsub
        return gv.at[pl.ds(sub * h, h), core, pos_y(off)]

    last_axis = {"o": along_z, "v": along_y}

    def run(stage, sizes, axis, block, nsubs, forward):
        plans = {name: ring_plan(sizes[name], nsubs) for name in ("o", "v")}

        def send(name, e):
            dirn, k, sub = e
            ref = block(name, -dirn * (k - 1), sub)
            rcopy(ref, ref, t["ring" + name], t[stage + name][e], *axis[name](dirn)).start()

        for name in ("o", "v"):
            plane_arrived(name)
            for e in plans[name]:
                if e[1] == 1:
                    send(name, e)
        if forward:
            for name in ("o", "v"):
                forward(name, None)
        order = []
        for n in range(max(len(plans["o"]), len(plans["v"]))):
            for name in ("v", "o"):
                if n < len(plans[name]):
                    order.append((name, plans[name][n]))
        for name, e in order:
            dirn, k, sub = e
            ref = block(name, -dirn * k, sub)
            i = t[stage + name][e]
            rcopy(ref, ref, i, i, g, b).wait_recv()
            nxt = (dirn, k + 1, sub)
            if nxt in plans[name]:
                send(name, nxt)
            if forward:
                forward(name, e)

    def sibling(name, e):
        if e is None:
            ref = go.at[z, c] if name == "o" else gv.at[:, c, y]
        else:
            dirn, k, sub = e
            ref = last_block(name, -dirn * k, sub, c)
        i = t["sib" + name]
        rcopy(ref, ref, i, i, sib, b).start()

    def from_sibling(name):
        ref = bufs[name].at[:, 1 - c]
        i = t["sib" + name]
        rcopy(ref, ref, i, i, g, b).wait_recv()

    run(
        "last",
        {"o": d.Z, "v": d.Y},
        last_axis,
        lambda name, off, sub: last_block(name, off, sub, c),
        nsub,
        sibling,
    )
    from_sibling("o")

    def tiles_of(ref, i):
        return ref[i // 2, lax.rem(i, 2)].reshape(d.K, TW, TW)

    def virtual_slot(kk):
        at = lax.rem(b // d.HP + kk, d.NT)
        j = lax.rem((g + d.NG - at) * 7, d.NG)
        row = owner_ref[j]
        tiles = tiles_of(gv, row)
        left = jnp.concatenate([tiles[s] for s in range(d.K)], axis=1)
        right = jnp.concatenate(
            [bm[lax.rem(row + voff_ref[s], d.NT)] for s in range(d.K)], axis=0
        )
        value = jnp.dot(left, right, preferred_element_type=F32).astype(BF16)
        for h in range(d.HP):
            to = at * d.HP + h
            rbuf[to] = value[h * d.CH : (h + 1) * d.CH]

            @pl.when(to != b)
            def _():
                rcopy(rbuf.at[to], rb.at[b], t["R"], t["R"], g, to).start()

            @pl.when(to == b)
            def _():
                rb[b] = value[h * d.CH : (h + 1) * d.CH]

    def occupied_slot(kk):
        at = lax.rem(b // d.HP + kk, d.NT)
        j = lax.rem(at + 7 * g, d.NG)
        col = owner_ref[j]
        lefts, rights = [], []
        for s in range(d.K):
            i = lax.rem(col - ooff_ref[s] + d.NT, d.NT)
            lefts.append(bt[i])
            rows = go[i // 2, lax.rem(i, 2)].reshape(d.K, TW, TW)[s]
            rights.append(rows)
        value = jnp.dot(
            jnp.concatenate(lefts, axis=1),
            jnp.concatenate(rights, axis=0),
            preferred_element_type=F32,
        ).astype(BF16)
        lbuf[j] = value

        for h in range(d.HP):
            to = at * d.HP + h
            src = lbuf.at[j, pl.ds(h * d.CH, d.CH)]

            @pl.when((to != b) | (j != g))
            def _():
                rcopy(src, lb.at[b], t["Lb"], t["Lb"], j, to).start()

            @pl.when((to == b) & (j == g))
            def _():
                lb[b] = value[h * d.CH : (h + 1) * d.CH]

    steps = {"L": occupied_slot, "R": virtual_slot}
    for what, lo, hi in SCHEDULE:
        if what == "R":
            from_sibling("v")

        @pl.loop(lo * d.NT // 16, hi * d.NT // 16, unroll=2)
        def _(kk):
            steps[what](kk)

    for name in ("o", "v"):
        plane_bytes(name).wait_send()
        ref = bufs[name].at[:, c]
        rcopy(ref, ref, t["sib" + name], t["sib" + name], g, b).wait_send()
        ref = bufs[name].at[pl.ds(0, d.Z - 1), c] if name == "o" else bufs[name].at[:, c, pl.ds(0, d.Y - 1)]
        rcopy(ref, ref, t["ring" + name], t["ring" + name], g, b).wait_send()

    def wait_all(ref, n, name):
        part = ref.at[pl.ds(0, n)]
        cp = rcopy(part, part, t[name], t[name], g, b)
        cp.wait_send()
        cp.wait_recv()

    wait_all(rb, d.NB - 1, "R")

    @pl.when(source != g)
    def _():
        wait_all(lb, d.NB, "Lb")

    @pl.when(source == g)
    def _():
        wait_all(lb, d.NB - 1, "Lb")

    n16 = d.NB * 16
    prod = jnp.zeros((n16, n16), F32)
    for r in range(d.CH // 16):
        left = lb[:, 16 * r : 16 * r + 16, :].reshape(n16, TW)
        right = rb[:, 16 * r : 16 * r + 16, :].reshape(n16, TW)
        prod = prod + lax.dot_general(
            left, right, (((1,), (1,)), ((), ())), preferred_element_type=F32
        )
    ii = lax.broadcasted_iota(jnp.int32, (n16, n16), 0)
    jj = lax.broadcasted_iota(jnp.int32, (n16, n16), 1)
    prod = jnp.where((ii & 15) == (jj & 15), prod, 0.0)
    folded = jnp.sum(prod.reshape(d.NB, 16, n16), axis=1)
    pick = (
        lax.broadcasted_iota(jnp.int32, (n16, TW), 0) // 16
        == lax.broadcasted_iota(jnp.int32, (n16, TW), 1)
    ).astype(F32)
    part = jnp.dot(
        folded, pick, precision=lax.Precision.HIGHEST, preferred_element_type=F32
    )
    for p in range(d.NB):
        s1[p] = part[p : p + 1]
    s1r[b] = s1[b]

    @pl.loop(1, d.NB)
    def _(k):
        q = lax.rem(b + k, d.NB)
        rcopy(s1.at[q], s1r.at[b], t["S1"], t["S1"], g, q).start()

    wait_all(s1r, d.NB - 1, "S1")
    s2[g] = jnp.sum(s1r[...], axis=0)

    @pl.loop(1, d.NG)
    def _(k):
        q = lax.rem(g + k, d.NG)
        rcopy(s2.at[g], s2.at[g], t["S2"], t["S2"], q, b).start()

    wait_all(s2, d.NG - 1, "S2")
    total = jnp.sum(s2[...], axis=0)
    out_ref[...] = total[:, : d.NB] * (1.0 / (d.NT * TW))


def make(d, nsub):
    t, nsem = layout(d, nsub)

    def body(integrals, mask, owner, otiles, ooff, vtiles, voff):
        vmem = pl.BlockSpec(memory_space=pltpu.VMEM)
        hbm = pl.BlockSpec(memory_space=pltpu.HBM)
        gshape = (d.Z, 2, d.Y, d.X, d.RPD, TW)
        return pl.pallas_call(
            functools.partial(kernel, d, nsub, t),
            out_shape=jax.ShapeDtypeStruct((1, d.NB), F32),
            in_specs=[hbm] * 7,
            out_specs=vmem,
            scratch_shapes=[
                pltpu.SMEM((d.NT, d.NT), jnp.int32),
                pltpu.SMEM((d.NT,), jnp.int32),
                pltpu.SMEM((d.K,), jnp.int32),
                pltpu.SMEM((d.K,), jnp.int32),
                pltpu.VMEM((1, d.NT * TW, TW), BF16),
                pltpu.VMEM(gshape, BF16),
                pltpu.VMEM(gshape, BF16),
                pltpu.VMEM((d.NT, TW, TW), BF16),
                pltpu.VMEM((d.NT, TW, TW), BF16),
                pltpu.VMEM((d.NB, d.CH, TW), BF16),
                pltpu.VMEM((d.NB, d.CH, TW), BF16),
                pltpu.VMEM((d.NT, TW, TW), BF16),
                pltpu.VMEM((d.NB, d.CH, TW), BF16),
                pltpu.VMEM((d.NB, 1, TW), F32),
                pltpu.VMEM((d.NB, 1, TW), F32),
                pltpu.VMEM((d.NG, 1, TW), F32),
                pltpu.SemaphoreType.DMA((nsem,)),
                pltpu.SemaphoreType.DMA((nsem,)),
            ],
            compiler_params=pltpu.CompilerParams(
                collective_id=0, has_side_effects=True, vmem_limit_bytes=60 << 20
            ),
        )(mask, owner, ooff, voff, integrals, otiles, vtiles)

    return body


def solution(mesh, x=4, kcount=8, nsub=4):
    d = Dims(mesh.shape["grp"], mesh.shape["blk"], x, kcount)
    in_specs = (
        P("blk", None, "grp"),
        P(),
        P(),
        P(("grp", "blk"), None),
        P(),
        P(("grp", "blk"), None),
        P(),
    )
    return jax.shard_map(
        make(d, nsub), mesh=mesh, in_specs=in_specs, out_specs=P("blk", None), check_vma=False
    )
```
